512 devices in a mesh: rows: 32 (over x, z), cols: 16 (over y, core).
Axes of the slice: x: 4, y: 8, z: 8, core: 2. Of those that a mesh axis runs over, the one named last changes fastest.
Arguments:
- points: float32 [3, 131072], P(None, 'rows'), as said below
- targets: float32 [16, 131072], P(None, 'rows'), may hold values from -6 to 6
- landmarks: int32 [256], replicated, may hold values from 0 to 131071
- neighbours: int32 [1024, 18], P('rows'), may hold values from 0 to 1023, as said below
- counts: int32 [1024], P('rows'), may hold values from 1 to 18
- core_inverse: float32 [256, 256], replicated, as said below
Outputs:
- solution: float32 [16, 131072], P(None, 'rows')
- residual: float32 [16, 131072], P(None, 'rows')
The draws below stay inside these ranges and needn't reach their ends.
Inputs may be any that keep to these rules, and one draw needn't show every extreme that they name: `neighbours`: for block b the first counts[b] entries are distinct blocks in ascending order, b among them, each within 12 blocks of b; b lists c exactly when c lists b; the remaining slots hold b. `points`: points of blocks that do not list each other are farther apart than 1. `core_inverse`: Symmetric; each diagonal entry exceeds the sum of the magnitudes of the other entries of its row.
All inputs are finite; a program needn't handle non-finite values.
Results may differ from the reference program's by a relative error of at most 0.0003.
Values sent between devices are 32-bit elements; how exact they have to be, the bound alone decides.
A program may use at most 64 MiB of HBM per device.

```python
import jax
import jax.numpy as jnp
from jax import lax

BLK = 128
OUT = 16
LAND = 256
MOST = 6
ITERS = 2
NBRS = 18
NB = 1024
NPTS = 131072


def layout(key):
    base = jax.random.fold_in(key, 11)
    keys = jax.random.split(base, 3)
    cell_sizes = jax.random.randint(keys[0], (NB,), 1, MOST + 1)
    cell_total = NB // MOST
    forced_start = jax.random.randint(keys[1], (), 0, cell_total - 2)
    cell_ids = jnp.arange(NB, dtype=jnp.int32)
    forced = (cell_ids >= forced_start) & (cell_ids < forced_start + 3)
    cell_sizes = jnp.where(forced, MOST, cell_sizes).astype(jnp.int32)
    cell_ends = jnp.cumsum(cell_sizes).astype(jnp.int32)
    block_ids = jnp.arange(NB, dtype=jnp.int32)
    block_cell = jnp.searchsorted(cell_ends, block_ids, side='right').astype(jnp.int32)
    block_lane = jax.random.randint(keys[2], (NB,), 0, 3)
    middle_first = cell_ends[forced_start + 1] - MOST
    block_lane = jnp.where(block_ids == middle_first, 1, block_lane).astype(jnp.int32)
    return (block_cell, block_lane)


def neighbour_table(key):
    block_cell, block_lane = layout(key)
    reach = 2 * MOST
    offset_row = jnp.arange(-reach, reach + 1, dtype=jnp.int32)
    block_ids = jnp.arange(NB, dtype=jnp.int32)
    partner = block_ids[:, None] + offset_row[None, :]
    inside = (partner >= 0) & (partner < NB)
    clipped = jnp.clip(partner, 0, NB - 1)
    valid = inside & (jnp.abs(block_cell[clipped] - block_cell[:, None]) <= 1)
    valid = valid & (jnp.abs(block_lane[clipped] - block_lane[:, None]) <= 1)
    scores = jnp.where(valid, 0, 2 * reach + 2) + jnp.arange(2 * reach + 1, dtype=jnp.int32)[None, :]
    order = jnp.argsort(scores, axis=1, stable=True)[:, :NBRS]
    chosen = jnp.take_along_axis(clipped, order, axis=1)
    kept = jnp.take_along_axis(valid, order, axis=1)
    listed = jnp.where(kept, chosen, block_ids[:, None]).astype(jnp.int32)
    amounts = jnp.sum(valid.astype(jnp.int32), axis=1).astype(jnp.int32)
    return (listed, amounts)


def draw_neighbours(key, part):
    return neighbour_table(key)[0]


def draw_counts(key, part):
    return neighbour_table(key)[1]


def draw_points(key, part):
    block_cell, block_lane = layout(key)
    jitter = jax.random.uniform(jax.random.fold_in(key, 23), (3, NPTS), dtype=jnp.float32)
    owner_block = jnp.arange(NPTS, dtype=jnp.int32) // BLK
    first_coord = block_cell[owner_block].astype(jnp.float32) + jitter[0]
    second_coord = block_lane[owner_block].astype(jnp.float32) + jitter[1]
    return jnp.stack([first_coord, second_coord, jitter[2]], axis=0).astype(jnp.float32)


def draw_core_inverse(key, part):
    first_key, second_key = jax.random.split(jax.random.fold_in(key, 31))
    raw_part = jax.random.uniform(first_key, (LAND, LAND), dtype=jnp.float32, minval=-1.0, maxval=1.0) * (9.6 / (LAND - 1))
    mirror = 0.5 * (raw_part + raw_part.T)
    diagonal = jnp.exp(jax.random.uniform(second_key, (LAND,), dtype=jnp.float32, minval=jnp.log(12.0), maxval=jnp.log(40.0)))
    identity = jnp.eye(LAND, dtype=jnp.float32)
    return (mirror * (1.0 - identity) + identity * diagonal[None, :]).astype(jnp.float32)


def set_ends(array, own_key, least, largest):
    index_at = [jax.random.randint(jax.random.fold_in(own_key, axis), (), 0, length) for axis, length in enumerate(array.shape)]
    main_axis = array.shape.index(max(array.shape))
    neighbour = index_at[:main_axis] + [(index_at[main_axis] + 1) % array.shape[main_axis]] + index_at[main_axis + 1:]
    return array.at[tuple(index_at)].set(least).at[tuple(neighbour)].set(largest)


def shard_levels(own_key, dims, cuts, low, top_value):
    def one(axis_at, blocks):
        steps = jax.random.uniform(jax.random.fold_in(jax.random.fold_in(own_key, 6), axis_at), (blocks,), jnp.float32, low / len(cuts), top_value / len(cuts))
        return jnp.repeat(jnp.exp(steps), dims[axis_at] // blocks).reshape((-1,) + (1,) * (len(dims) - axis_at - 1))

    gain = one(*cuts[0])
    for cut in cuts[1:]:
        gain = gain * one(*cut)
    return gain


def noise(stream_key, shape, spread, most, cuts=(), kind=jnp.bfloat16):
    result = jax.random.normal(stream_key, shape, jnp.float32) * spread
    if len(cuts) > 0:
        result = shard_levels(stream_key, shape, cuts, -0.22, 0.18) * result
    return jnp.clip(result, min=-most, max=most).astype(kind)


def setup_inputs(seed: int = 0) -> dict:
    streams_of = jax.random.split(jax.random.key(seed), 7)
    return {
        "points": draw_points(jax.random.fold_in(streams_of[6], 71), 0),
        "targets": noise(streams_of[1], (OUT, NPTS), 1.0, 6.0, ((1, 32),), jnp.float32),
        "landmarks": set_ends(jax.random.randint(streams_of[2], (LAND,), 0, NPTS), jax.random.fold_in(streams_of[2], 1), 0, NPTS - 1).astype(jnp.int32),
        "neighbours": draw_neighbours(jax.random.fold_in(streams_of[6], 71), 0),
        "counts": draw_counts(jax.random.fold_in(streams_of[6], 71), 0),
        "core_inverse": draw_core_inverse(jax.random.fold_in(streams_of[6], 71), 0),
    }


kernel_scale = 0.03125
ridge_shift = 1.0

def wendland(squared):
    distance = jnp.sqrt(squared)
    remain = jnp.maximum(1.0 - distance, 0.0)
    return remain * remain * remain * remain * (4.0 * distance + 1.0)

def squared_gap(first_pts, second_pts):
    offsets = first_pts[:, :, None] - second_pts[:, None, :]
    return lax.optimization_barrier(jnp.sum(offsets * offsets, axis=0))

def kernel_apply(points, neighbours, counts, vector):
    blocks = points.reshape(3, NB, BLK)
    values = vector.reshape(OUT, NB, BLK)
    groups = jnp.arange(NB, dtype=jnp.int32).reshape(NB // 16, 16)
    slot_ids = jnp.arange(NBRS, dtype=jnp.int32)

    def one_group(row_ids):
        nearby_ids = neighbours[row_ids]
        usable = (slot_ids[None, :] < counts[row_ids][:, None]).astype(points.dtype)
        row_points = blocks[:, row_ids]
        col_points = blocks[:, nearby_ids]
        offsets = row_points[:, :, None, :, None] - col_points[:, :, :, None, :]
        kernel_tiles = wendland(lax.optimization_barrier(jnp.sum(offsets * offsets, axis=0))) * usable[:, :, None, None]
        return jnp.einsum('orsn,rsmn->orm', values[:, nearby_ids], kernel_tiles, precision=lax.Precision.HIGHEST)
    mapped = lax.map(one_group, groups)
    return jnp.transpose(mapped, (1, 0, 2, 3)).reshape(OUT, NPTS)

def reference(points, targets, landmarks, neighbours, counts, core_inverse):
    landmark_coords = points[:, landmarks]
    grouped_points = jnp.transpose(points.reshape(3, NB // 16, 16 * BLK), (1, 0, 2))

    def project(vector):
        grouped_vector = jnp.transpose(vector.reshape(OUT, NB // 16, 16 * BLK), (1, 0, 2))

        def piece(pair):
            kernel_part = wendland(squared_gap(landmark_coords, pair[0]))
            return jnp.dot(pair[1], kernel_part.T, precision=lax.Precision.HIGHEST)
        return lax.optimization_barrier(jnp.sum(lax.map(piece, (grouped_points, grouped_vector)), axis=0))

    def expand(weights):

        def piece(group_pts):
            kernel_part = wendland(squared_gap(landmark_coords, group_pts))
            return jnp.dot(weights, kernel_part, precision=lax.Precision.HIGHEST)
        mapped = lax.map(piece, grouped_points)
        return jnp.transpose(mapped, (1, 0, 2)).reshape(OUT, NPTS)

    def precondition(vector):
        projected = kernel_scale * project(vector)
        weights = jnp.dot(projected, core_inverse, precision=lax.Precision.HIGHEST)
        return vector - kernel_scale * expand(weights)

    def operate(vector):
        return kernel_scale * kernel_apply(points, neighbours, counts, vector) + ridge_shift * vector
    solution = jnp.zeros_like(targets)
    residual = targets
    preconditioned = precondition(residual)
    direction = preconditioned
    current = lax.optimization_barrier(jnp.sum(residual * preconditioned, axis=1))
    for iteration in range(ITERS):
        applied = operate(direction)
        step_size = current / lax.optimization_barrier(jnp.sum(direction * applied, axis=1))
        solution = solution + step_size[:, None] * direction
        residual = residual - step_size[:, None] * applied
        if iteration + 1 < ITERS:
            preconditioned = precondition(residual)
            following = lax.optimization_barrier(jnp.sum(residual * preconditioned, axis=1))
            direction = preconditioned + (following / current)[:, None] * direction
            current = following
    return (solution, residual)
```

```python
import jax
import jax.numpy as jnp
from jax import lax
from jax.sharding import PartitionSpec as P

MOST = 6
REACH = 2 * MOST

kernel_scale = 0.03125
ridge_shift = 1.0


def wendland(squared):
    distance = jnp.sqrt(squared)
    remain = jnp.maximum(1.0 - distance, 0.0)
    square = remain * remain
    return square * square * (4.0 * distance + 1.0)


def kernel_matrix(first_pts, second_pts):
    squared = 0.0
    for dim in range(3):
        offsets = first_pts[dim][:, None] - second_pts[dim][None, :]
        squared = squared + offsets * offsets
    return wendland(squared)


def product(first, second):
    return jnp.dot(first, second, precision=lax.Precision.HIGHEST)


def total(part):
    part = jnp.sum(lax.all_gather(part, "cols"), axis=0)
    return jnp.sum(lax.all_gather(part, "rows"), axis=0)


def extended(cells, width):
    count = lax.axis_size("rows")
    tail = cells[:, cells.shape[1] - width :]
    head = cells[:, :width]
    return jnp.concatenate(
        [
            lax.ppermute(tail, "rows", [(i, i + 1) for i in range(count - 1)]),
            cells,
            lax.ppermute(head, "rows", [(i + 1, i) for i in range(count - 1)]),
        ],
        axis=1,
    )


def body(points, targets, landmarks, neighbours, counts, core_inverse):
    col_count = lax.axis_size("cols")
    row_count = lax.axis_size("rows")
    row_index = lax.axis_index("rows")
    col_index = lax.axis_index("cols")
    slab = points.shape[1]
    block = slab // neighbours.shape[0]
    share = slab // col_count
    outs = targets.shape[0]
    halo = REACH * block
    window = share + 2 * halo

    local_ids = landmarks - row_index * slab
    present = (local_ids >= 0) & (local_ids < slab)
    picked = jnp.take(points, jnp.clip(local_ids, 0, slab - 1), axis=1)
    picked = jnp.where(present[None, :], picked, 0.0)
    marks = jnp.sum(lax.all_gather(picked, "rows"), axis=0)

    wide = extended(jnp.concatenate([points, targets], axis=0), halo)
    place = jnp.arange(slab + 2 * halo, dtype=jnp.int32) - halo
    place = place + row_index * slab
    valid = ((place >= 0) & (place < slab * row_count)).astype(jnp.float32)[None, :]
    wide_points = wide[:3]
    wide_targets = wide[3:]

    def near(array):
        return lax.dynamic_slice_in_dim(array, col_index * share, window, 1)

    def own(array):
        return lax.dynamic_slice_in_dim(array, halo + col_index * share, share, 1)

    marks_wide = kernel_scale * kernel_matrix(marks, wide_points)
    band = kernel_scale * kernel_matrix(near(wide_points), own(wide_points))
    marks_own = own(marks_wide).T

    def operate(vector):
        return product(near(vector), band) + ridge_shift * own(vector)

    def dots(first, second):
        return jnp.sum(first * second, axis=1, keepdims=True)

    first_own = own(wide_targets)
    sums = total(
        jnp.concatenate(
            [product(first_own, marks_own), dots(first_own, first_own)], axis=1
        )
    )
    u0 = sums[:, :-1]
    w0 = product(u0, core_inverse)
    rz0 = sums[:, -1:] - dots(w0, u0)
    z0 = (wide_targets - product(w0, marks_wide)) * valid
    q0 = operate(z0)
    q0_wide = extended(lax.all_gather(q0, "cols", axis=1, tiled=True), halo)
    z0_own = own(z0)
    sums = total(jnp.concatenate([product(q0, marks_own), dots(z0_own, q0)], axis=1))
    curve0 = sums[:, -1:]
    alpha0 = rz0 / curve0
    u1 = u0 - alpha0 * sums[:, :-1]
    r1 = wide_targets - alpha0 * q0_wide
    z1 = (r1 - product(product(u1, core_inverse), marks_wide)) * valid
    w1 = operate(z1)
    z1_own = own(z1)
    r1_own = own(r1)
    sums = total(
        jnp.concatenate(
            [dots(r1_own, z1_own), dots(z1_own, w1), dots(z1_own, q0) + dots(z0_own, w1)],
            axis=1,
        )
    )
    w1_slab = lax.all_gather(w1, "cols", axis=1, tiled=True)
    rz1 = sums[:, :1]
    beta = rz1 / rz0
    curve1 = sums[:, 1:2] + beta * (sums[:, 2:] + beta * curve0)
    alpha1 = rz1 / curve1

    def inner(array):
        return array[:, halo : halo + slab]

    z0_slab = inner(z0)
    solution = alpha0 * z0_slab + alpha1 * (inner(z1) + beta * z0_slab)
    residual = inner(r1) - alpha1 * (w1_slab + beta * inner(q0_wide))
    return (solution, residual)


def solution(mesh):
    placed = (P(None, "rows"), P(None, "rows"), P(), P("rows", None), P("rows"), P())
    return jax.shard_map(
        body,
        mesh=mesh,
        in_specs=placed,
        out_specs=(P(None, "rows"), P(None, "rows")),
        check_vma=False,
    )
```

```python
import functools

import jax
import jax.numpy as jnp
from jax import lax
from jax.experimental import pallas as pl
from jax.experimental.pallas import tpu as pltpu
from jax.sharding import PartitionSpec as P

MOST = 6
REACH = 2 * MOST

kernel_scale = 0.03125
ridge_shift = 1.0

F32 = jnp.float32
BF16 = jnp.bfloat16
MESH = pl.DeviceIdType.MESH
PTS = 8


def halves(value):
    high = value.astype(BF16)
    return high, (value - high.astype(F32)).astype(BF16)


def product(value, high, low):
    rows = value.shape[0]
    value_high, value_low = halves(value)
    both = jnp.concatenate([value_high, value_low], axis=0)
    first = jnp.dot(both, high, preferred_element_type=F32)
    second = jnp.dot(value_high, low, preferred_element_type=F32)
    return first[:rows] + (first[rows:] + second)


def kernel_rows(column, lanes):
    squared = None
    for dim in range(3):
        offsets = column[:, dim : dim + 1] - lanes[dim : dim + 1, :]
        term = offsets * offsets
        squared = term if squared is None else squared + term
    distance = squared * lax.rsqrt(jnp.maximum(squared, 1e-30))
    remain = jnp.maximum(1.0 - distance, 0.0)
    square = remain * remain
    return (square * square) * ((4.0 * kernel_scale) * distance + kernel_scale)


def solve_kernel(
    rows,
    cols,
    halo,
    data_in,
    picked,
    core,
    sol_out,
    res_out,
    data,
    marks,
    column,
    band_high,
    band_low,
    mark_high,
    mark_low,
    own_high,
    own_low,
    core_high,
    core_low,
    near_z,
    z_first,
    z_next,
    r_next,
    q_send,
    q_first,
    q_next,
    part_send,
    part_recv,
    row_send,
    row_recv,
    all_send,
    all_recv,
    halo_send_sem,
    halo_recv_sem,
    mark_send_sem,
    mark_recv_sem,
    q_send_sem,
    q_recv_sem,
    q2_send_sem,
    q2_recv_sem,
    part_send_sem,
    part_recv_sem,
    row_send_sem,
    row_recv_sem,
    all_send_sem,
    all_recv_sem,
):
    r = lax.axis_index("rows")
    c = lax.axis_index("cols")
    width = data.shape[2]
    outs = data.shape[1] - PTS
    near = 2 * halo + 1
    piece = 64
    group = outs // cols

    def target(row, col):
        return (row, col)

    def col_peer(step):
        return lax.rem(c + step, cols)

    def row_peer(step):
        return lax.rem(r + step, rows)

    def loop(count, fn, start=0):
        def step(i, carry):
            fn(i)
            return carry

        lax.fori_loop(start, count, step, 0)

    def edge_peers(fn):
        def one(k):
            @pl.when((r < rows - 1) & (k <= c + halo - cols))
            def _():
                fn(k, r + 1, k, halo + cols + k)

            @pl.when((r > 0) & (k >= c))
            def _():
                fn(halo + k, r - 1, cols - halo + k, k)

        loop(halo, one)

    barrier = pltpu.get_barrier_semaphore()

    def greet(row, col):
        pl.semaphore_signal(barrier, inc=1, device_id=target(row, col), device_id_type=MESH)

    loop(cols, lambda i: greet(r, col_peer(i)), 1)
    loop(rows, lambda i: greet(row_peer(i), c), 1)
    edge_peers(lambda index, row, col, slot: greet(row, col))
    right_extra = jnp.where(r < rows - 1, jnp.maximum(c + halo - cols + 1, 0), 0)
    left_extra = jnp.where(r > 0, jnp.maximum(halo - c, 0), 0)
    pl.semaphore_wait(barrier, cols + rows - 2 + right_extra + left_extra)

    def halo_right():
        return pltpu.make_async_remote_copy(
            src_ref=data_in.at[pl.ds(cols - halo, halo)],
            dst_ref=data.at[pl.ds(0, halo)],
            send_sem=halo_send_sem.at[0],
            recv_sem=halo_recv_sem.at[0],
            device_id=target(jnp.minimum(r + 1, rows - 1), c),
            device_id_type=MESH,
        )

    def halo_left():
        return pltpu.make_async_remote_copy(
            src_ref=data_in.at[pl.ds(0, halo)],
            dst_ref=data.at[pl.ds(halo + cols, halo)],
            send_sem=halo_send_sem.at[1],
            recv_sem=halo_recv_sem.at[1],
            device_id=target(jnp.maximum(r - 1, 0), c),
            device_id_type=MESH,
        )

    def mark_copy(peer, slot):
        return pltpu.make_async_remote_copy(
            src_ref=picked,
            dst_ref=marks.at[slot],
            send_sem=mark_send_sem.at[peer],
            recv_sem=mark_recv_sem.at[slot],
            device_id=target(peer, c),
            device_id_type=MESH,
        )

    loop(rows, lambda i: mark_copy(row_peer(i), r).start(), 1)

    @pl.when(r < rows - 1)
    def _():
        halo_right().start()

    @pl.when(r > 0)
    def _():
        halo_left().start()

    def keep(i):
        data[halo + i] = data_in[i]

    loop(cols, keep)
    marks[r] = picked[...]
    high, low = halves(core[...])
    core_high[...] = high
    core_low[...] = low

    @pl.when(r == 0)
    def _():
        data[0:halo] = jnp.zeros((halo,) + data.shape[1:], F32)

    @pl.when(r == rows - 1)
    def _():
        data[halo + cols : 2 * halo + cols] = jnp.zeros((halo,) + data.shape[1:], F32)

    @pl.when(r > 0)
    def _():
        halo_right().wait_recv()

    @pl.when(r < rows - 1)
    def _():
        halo_left().wait_recv()

    own = c + halo

    def fill(lanes, put):
        def one(i):
            at = pl.multiple_of(i * piece, piece)
            high, low = halves(kernel_rows(column[pl.ds(at, piece), :], lanes))
            put(at, high, low)

        for i in range(width // piece):
            one(i)

    own_lanes = data[own, 0:PTS, :]

    def band_slot(i):
        column[...] = jnp.transpose(data[c + i, 0:PTS, :])

        def put(at, high, low):
            band_high[i, pl.ds(at, piece), :] = high
            band_low[i, pl.ds(at, piece), :] = low

        fill(own_lanes, put)

    loop(near, band_slot)

    loop(rows, lambda i: mark_copy(r, row_peer(i)).wait_recv(), 1)
    mark_lanes = jnp.sum(marks[...], axis=0)
    mark_wide = jnp.concatenate(
        [mark_lanes, jnp.zeros((PTS - mark_lanes.shape[0], width), F32)], axis=0
    )
    column[...] = jnp.transpose(own_lanes)

    def put_own(at, high, low):
        own_high[pl.ds(at, piece), :] = high
        own_low[pl.ds(at, piece), :] = low

    fill(mark_wide, put_own)
    column[...] = jnp.transpose(mark_wide)

    def mark_slot(i):
        def put(at, high, low):
            mark_high[i, pl.ds(at, piece), :] = high
            mark_low[i, pl.ds(at, piece), :] = low

        fill(data[i, 0:PTS, :], put)

    def part_copy(k, peer, slot):
        return pltpu.make_async_remote_copy(
            src_ref=part_send.at[k, peer],
            dst_ref=part_recv.at[k, slot],
            send_sem=part_send_sem.at[peer],
            recv_sem=part_recv_sem.at[k, slot],
            device_id=target(r, peer),
            device_id_type=MESH,
        )

    def row_copy(k, peer, slot):
        return pltpu.make_async_remote_copy(
            src_ref=row_send.at[k],
            dst_ref=row_recv.at[k, slot],
            send_sem=row_send_sem.at[peer],
            recv_sem=row_recv_sem.at[k, slot],
            device_id=target(peer, c),
            device_id_type=MESH,
        )

    def all_copy(k, peer, slot):
        return pltpu.make_async_remote_copy(
            src_ref=all_send.at[k],
            dst_ref=all_recv.at[k, slot],
            send_sem=all_send_sem.at[peer],
            recv_sem=all_recv_sem.at[k, slot],
            device_id=target(r, peer),
            device_id_type=MESH,
        )

    def total(k, value, first_work, second_work, third_work):
        for p in range(cols):
            part_send[k, p] = value[p * group : (p + 1) * group, :]
        loop(cols, lambda i: part_copy(k, col_peer(i), c).start(), 1)
        part_recv[k, c] = part_send[k, c]
        first_work()
        loop(cols, lambda i: part_copy(k, c, col_peer(i)).wait_recv(), 1)
        row_part = jnp.sum(part_recv[k], axis=0)
        row_send[k] = row_part
        row_recv[k, r] = row_part
        loop(rows, lambda i: row_copy(k, row_peer(i), r).start(), 1)
        second_work()
        loop(rows, lambda i: row_copy(k, r, row_peer(i)).wait_recv(), 1)
        whole = jnp.sum(row_recv[k], axis=0)
        all_send[k] = whole
        all_recv[k, c] = whole
        loop(cols, lambda i: all_copy(k, col_peer(i), c).start(), 1)
        third_work()
        loop(cols, lambda i: all_copy(k, c, col_peer(i)).wait_recv(), 1)
        loop(cols, lambda i: part_copy(k, col_peer(i), c).wait_send(), 1)
        loop(rows, lambda i: row_copy(k, row_peer(i), r).wait_send(), 1)
        loop(cols, lambda i: all_copy(k, col_peer(i), c).wait_send(), 1)
        return jnp.concatenate([all_recv[k, p] for p in range(cols)], axis=0)

    def message(body, scalars):
        lane = lax.broadcasted_iota(jnp.int32, (outs, 128), 1)
        tail = jnp.zeros((outs, 128), F32)
        for index, scalar in enumerate(scalars):
            tail = jnp.where(lane == index, scalar, tail)
        return jnp.concatenate([body, tail], axis=1)

    def dots(first, second):
        return jnp.sum(first * second, axis=1, keepdims=True)

    def nothing():
        pass

    slots = cols + 2 * halo
    cut_first = slots // 3
    cut_second = (2 * slots) // 3

    own_targets = data[own, PTS:, :]
    sums = total(
        0,
        message(
            product(own_targets, own_high[...], own_low[...]), [dots(own_targets, own_targets)]
        ),
        lambda: loop(cut_first, mark_slot),
        lambda: loop(cut_second, mark_slot, cut_first),
        lambda: loop(slots, mark_slot, cut_second),
    )
    u0 = sums[:, :width]
    w0 = product(u0, core_high[...], core_low[...])
    rz0 = sums[:, width : width + 1] - dots(w0, u0)

    def apply_near(make):
        def step(i, running):
            slot = c + i
            place = r * cols + slot - halo
            valid = (place >= 0) & (place < rows * cols)
            value = jnp.where(valid, make(slot), 0.0)
            near_z[i] = value
            return running + product(value, band_high[i], band_low[i])

        image = lax.fori_loop(0, near, step, jnp.zeros((outs, width), F32))
        return image + ridge_shift * near_z[halo]

    def first_z(slot):
        return data[slot, PTS:, :] - product(w0, mark_high[slot], mark_low[slot])

    q0 = apply_near(first_z)
    z0_own = near_z[halo]
    q_send[0] = q0
    q_first[own] = q0

    def q_copy(index, row, col, slot):
        return pltpu.make_async_remote_copy(
            src_ref=q_send.at[0],
            dst_ref=q_first.at[slot],
            send_sem=q_send_sem.at[index],
            recv_sem=q_recv_sem.at[slot],
            device_id=target(row, col),
            device_id_type=MESH,
        )

    def send_index(peer):
        return 2 * halo + peer

    image_message = message(product(q0, own_high[...], own_low[...]), [dots(z0_own, q0)])

    def send_first():
        edge_peers(
            lambda index, row, col, slot: q_copy(
                index, row, col, jnp.where(row > r, c - cols + halo, halo + cols + c)
            ).start()
        )
        loop(cols, lambda i: q_copy(send_index(col_peer(i)), r, col_peer(i), own).start(), 1)

    def first_slab(i):
        z_first[i] = first_z(halo + i)

    def take_first():
        edge_peers(lambda index, row, col, slot: q_copy(index, row, col, slot).wait_recv())
        loop(
            cols,
            lambda i: q_copy(send_index(c), r, c, halo + col_peer(i)).wait_recv(),
            1,
        )

    sums = total(
        1, image_message, send_first, lambda: loop(cols, first_slab), take_first
    )
    edge_peers(lambda index, row, col, slot: q_copy(index, row, col, slot).wait_send())
    loop(cols, lambda i: q_copy(send_index(col_peer(i)), r, col_peer(i), own).wait_send(), 1)

    curve0 = sums[:, width : width + 1]
    alpha0 = rz0 / curve0
    u1 = u0 - alpha0 * sums[:, :width]
    w1 = product(u1, core_high[...], core_low[...])

    def next_r(slot):
        return data[slot, PTS:, :] - alpha0 * q_first[slot]

    def next_z(slot):
        return next_r(slot) - product(w1, mark_high[slot], mark_low[slot])

    image = apply_near(next_z)
    z1_own = near_z[halo]
    r1_own = next_r(own)
    q_send[1] = image
    q_next[c] = image

    def q2_copy(peer, slot):
        return pltpu.make_async_remote_copy(
            src_ref=q_send.at[1],
            dst_ref=q_next.at[slot],
            send_sem=q2_send_sem.at[peer],
            recv_sem=q2_recv_sem.at[slot],
            device_id=target(r, peer),
            device_id_type=MESH,
        )

    def next_slab(i):
        residual = next_r(halo + i)
        r_next[i] = residual
        z_next[i] = residual - product(w1, mark_high[halo + i], mark_low[halo + i])

    sums = total(
        2,
        message(
            jnp.zeros((outs, width), F32),
            [dots(r1_own, z1_own), dots(z1_own, image), dots(z1_own, q0) + dots(z0_own, image)],
        ),
        lambda: loop(cols, lambda i: q2_copy(col_peer(i), c).start(), 1),
        lambda: loop(cols, next_slab),
        lambda: loop(cols, lambda i: q2_copy(c, col_peer(i)).wait_recv(), 1),
    )
    rz1 = sums[:, width : width + 1]
    beta = rz1 / rz0
    curve1 = sums[:, width + 1 : width + 2] + beta * (
        sums[:, width + 2 : width + 3] + beta * curve0
    )
    alpha1 = rz1 / curve1

    def finish(i):
        at = pl.ds(pl.multiple_of(i * width, width), width)
        first = z_first[i]
        sol_out[:, at] = alpha0 * first + alpha1 * (z_next[i] + beta * first)
        res_out[:, at] = r_next[i] - alpha1 * (q_next[i] + beta * q_first[halo + i])

    loop(cols, finish)

    loop(cols, lambda i: q2_copy(col_peer(i), c).wait_send(), 1)
    loop(rows, lambda i: mark_copy(row_peer(i), r).wait_send(), 1)

    @pl.when(r < rows - 1)
    def _():
        halo_right().wait_send()

    @pl.when(r > 0)
    def _():
        halo_left().wait_send()


def body(points, targets, landmarks, neighbours, counts, core_inverse):
    cols = lax.axis_size("cols")
    rows = lax.axis_size("rows")
    row_index = lax.axis_index("rows")
    slab = points.shape[1]
    block = slab // neighbours.shape[0]
    width = slab // cols
    outs = targets.shape[0]
    land = landmarks.shape[0]
    halo = -(-REACH * block // width)
    near = 2 * halo + 1
    slots = cols + 2 * halo

    local_ids = landmarks - row_index * slab
    present = (local_ids >= 0) & (local_ids < slab)
    picked = jnp.take(points, jnp.clip(local_ids, 0, slab - 1), axis=1)
    picked = jnp.where(present[None, :], picked, 0.0)
    picked = jnp.concatenate([picked, jnp.zeros((1, land), F32)], axis=0)
    lines = PTS + outs
    data = jnp.concatenate([points, jnp.zeros((PTS - 3, slab), F32), targets], axis=0)
    data = data.reshape(lines, cols, width).transpose(1, 0, 2)

    vmem = pltpu.VMEM
    dma = pltpu.SemaphoreType.DMA
    group = outs // cols
    wide = land + 128
    scratch = [
        vmem((slots, lines, width), F32),
        vmem((rows, 4, land), F32),
        vmem((width, PTS), F32),
        vmem((near, width, width), BF16),
        vmem((near, width, width), BF16),
        vmem((slots, land, width), BF16),
        vmem((slots, land, width), BF16),
        vmem((width, land), BF16),
        vmem((width, land), BF16),
        vmem((land, land), BF16),
        vmem((land, land), BF16),
        vmem((near, outs, width), F32),
        vmem((cols, outs, width), F32),
        vmem((cols, outs, width), F32),
        vmem((cols, outs, width), F32),
        vmem((2, outs, width), F32),
        vmem((slots, outs, width), F32),
        vmem((cols, outs, width), F32),
        vmem((3, cols, group, wide), F32),
        vmem((3, cols, group, wide), F32),
        vmem((3, group, wide), F32),
        vmem((3, rows, group, wide), F32),
        vmem((3, group, wide), F32),
        vmem((3, cols, group, wide), F32),
        dma((2,)),
        dma((2,)),
        dma((rows,)),
        dma((rows,)),
        dma((slots,)),
        dma((slots,)),
        dma((cols,)),
        dma((cols,)),
        dma((cols,)),
        dma((3, cols)),
        dma((rows,)),
        dma((3, rows)),
        dma((cols,)),
        dma((3, cols)),
    ]
    shape = jax.ShapeDtypeStruct((outs, slab), F32)
    return tuple(
        pl.pallas_call(
            functools.partial(solve_kernel, rows, cols, halo),
            out_shape=(shape, shape),
            in_specs=[pl.BlockSpec(memory_space=pltpu.VMEM)] * 3,
            out_specs=[pl.BlockSpec(memory_space=pltpu.VMEM)] * 2,
            scratch_shapes=scratch,
            compiler_params=pltpu.CompilerParams(
                collective_id=0,
                has_side_effects=True,
                vmem_limit_bytes=48 * 1024 * 1024,
            ),
        )(data, picked, core_inverse)
    )


def solution(mesh):
    placed = (P(None, "rows"), P(None, "rows"), P(), P("rows", None), P("rows"), P())
    return jax.shard_map(
        body,
        mesh=mesh,
        in_specs=placed,
        out_specs=(P(None, "rows"), P(None, "rows")),
        check_vma=False,
    )
```

```python
import functools

import jax
import jax.numpy as jnp
from jax import lax
from jax.experimental import pallas as pl
from jax.experimental.pallas import tpu as pltpu
from jax.sharding import PartitionSpec as P

MOST = 6
REACH = 2 * MOST

kernel_scale = 0.03125
ridge_shift = 1.0

F32 = jnp.float32
BF16 = jnp.bfloat16
MESH = pl.DeviceIdType.MESH
PTS = 8


def halves(value):
    high = value.astype(BF16)
    return high, (value - high.astype(F32)).astype(BF16)


def product(value, high, low):
    rows = value.shape[0]
    value_high, value_low = halves(value)
    both = jnp.concatenate([value_high, value_low], axis=0)
    first = jnp.dot(both, high, preferred_element_type=F32)
    second = jnp.dot(value_high, low, preferred_element_type=F32)
    return first[:rows] + (first[rows:] + second)


def kernel_rows(column, lanes):
    squared = None
    for dim in range(3):
        offsets = column[:, dim : dim + 1] - lanes[dim : dim + 1, :]
        term = offsets * offsets
        squared = term if squared is None else squared + term
    distance = squared * lax.rsqrt(jnp.maximum(squared, 1e-30))
    remain = jnp.maximum(1.0 - distance, 0.0)
    square = remain * remain
    return (square * square) * ((4.0 * kernel_scale) * distance + kernel_scale)


def solve_kernel(
    rows,
    cols,
    halo,
    data_in,
    picked,
    close,
    core,
    sol_out,
    res_out,
    data,
    marks,
    column,
    band_high,
    band_low,
    mark_high,
    mark_low,
    own_high,
    own_low,
    core_high,
    core_low,
    near_z,
    z_first,
    z_next,
    r_next,
    q_send,
    q_first,
    q_next,
    part_send,
    part_recv,
    row_send,
    row_recv,
    all_send,
    all_recv,
    small_send,
    small_recv,
    last_send,
    last_recv,
    halo_send_sem,
    halo_recv_sem,
    mark_send_sem,
    mark_recv_sem,
    q_send_sem,
    q_recv_sem,
    q2_send_sem,
    q2_recv_sem,
    part_send_sem,
    part_recv_sem,
    row_send_sem,
    row_recv_sem,
    all_send_sem,
    all_recv_sem,
):
    r = lax.axis_index("rows")
    c = lax.axis_index("cols")
    width = data.shape[2]
    outs = data.shape[1] - PTS
    near = 2 * halo + 1
    piece = 64
    group = outs // cols

    def target(row, col):
        return (row, col)

    def col_peer(step):
        return lax.rem(c + step, cols)

    def row_peer(step):
        return lax.rem(r + step, rows)

    def loop(count, fn, start=0):
        def step(i, carry):
            fn(i)
            return carry

        lax.fori_loop(start, count, step, 0)

    def edge_peers(fn):
        def one(k):
            @pl.when((r < rows - 1) & (k <= c + halo - cols))
            def _():
                fn(k, r + 1, k, halo + cols + k)

            @pl.when((r > 0) & (k >= c))
            def _():
                fn(halo + k, r - 1, cols - halo + k, k)

        loop(halo, one)

    barrier = pltpu.get_barrier_semaphore()

    def greet(row, col):
        pl.semaphore_signal(barrier, inc=1, device_id=target(row, col), device_id_type=MESH)

    loop(cols, lambda i: greet(r, col_peer(i)), 1)
    loop(rows, lambda i: greet(row_peer(i), c), 1)
    edge_peers(lambda index, row, col, slot: greet(row, col))
    right_extra = jnp.where(r < rows - 1, jnp.maximum(c + halo - cols + 1, 0), 0)
    left_extra = jnp.where(r > 0, jnp.maximum(halo - c, 0), 0)
    pl.semaphore_wait(barrier, cols + rows - 2 + right_extra + left_extra)

    def halo_right():
        return pltpu.make_async_remote_copy(
            src_ref=data_in.at[pl.ds(cols - halo, halo)],
            dst_ref=data.at[pl.ds(0, halo)],
            send_sem=halo_send_sem.at[0],
            recv_sem=halo_recv_sem.at[0],
            device_id=target(jnp.minimum(r + 1, rows - 1), c),
            device_id_type=MESH,
        )

    def halo_left():
        return pltpu.make_async_remote_copy(
            src_ref=data_in.at[pl.ds(0, halo)],
            dst_ref=data.at[pl.ds(halo + cols, halo)],
            send_sem=halo_send_sem.at[1],
            recv_sem=halo_recv_sem.at[1],
            device_id=target(jnp.maximum(r - 1, 0), c),
            device_id_type=MESH,
        )

    def mark_copy(peer, slot):
        return pltpu.make_async_remote_copy(
            src_ref=picked,
            dst_ref=marks.at[slot],
            send_sem=mark_send_sem.at[peer],
            recv_sem=mark_recv_sem.at[slot],
            device_id=target(peer, c),
            device_id_type=MESH,
        )

    mark_copy(row_peer(1), r).start()
    mark_copy(row_peer(rows - 1), r).start()
    loop(rows - 1, lambda i: mark_copy(row_peer(i), r).start(), 2)

    @pl.when(r < rows - 1)
    def _():
        halo_right().start()

    @pl.when(r > 0)
    def _():
        halo_left().start()

    def keep(i):
        data[halo + i] = data_in[i]

    loop(cols, keep)
    marks[r] = picked[...]
    high, low = halves(core[...])
    core_high[...] = high
    core_low[...] = low

    @pl.when(r == 0)
    def _():
        data[0:halo] = jnp.zeros((halo,) + data.shape[1:], F32)

    @pl.when(r == rows - 1)
    def _():
        data[halo + cols : 2 * halo + cols] = jnp.zeros((halo,) + data.shape[1:], F32)

    own = c + halo

    def fill(lanes, put):
        def one(i):
            at = pl.multiple_of(i * piece, piece)
            high, low = halves(kernel_rows(column[pl.ds(at, piece), :], lanes))
            put(at, high, low)

        for i in range(width // piece):
            one(i)

    own_lanes = data_in[c, 0:PTS, :]

    def band_slot(i):
        column[...] = jnp.transpose(data[c + i, 0:PTS, :])

        def put(at, high, low):
            band_high[i, pl.ds(at, piece), :] = high
            band_low[i, pl.ds(at, piece), :] = low

        fill(own_lanes, put)

    def widen(lanes):
        return jnp.concatenate([lanes, jnp.zeros((PTS - lanes.shape[0], width), F32)], axis=0)

    before = row_peer(rows - 1)
    after = row_peer(1)
    mark_copy(r, before).wait_recv()
    mark_copy(r, after).wait_recv()
    close_lanes = widen(marks[before] + picked[...] + marks[after])
    column[...] = jnp.transpose(own_lanes)
    close_row = close[0:1, :]

    def put_own(at, high, low):
        high = high * close_row.astype(BF16)
        low = low * close_row.astype(BF16)
        own_high[pl.ds(at, piece), :] = high
        own_low[pl.ds(at, piece), :] = low

    fill(close_lanes, put_own)

    def mark_slot(i):
        def put(at, high, low):
            mark_high[i, pl.ds(at, piece), :] = high
            mark_low[i, pl.ds(at, piece), :] = low

        fill(data[i, 0:PTS, :], put)

    def first_band():
        @pl.when(r > 0)
        def _():
            halo_right().wait_recv()

        @pl.when(r < rows - 1)
        def _():
            halo_left().wait_recv()

        loop(near, band_slot)

    def first_marks():
        loop(rows - 1, lambda i: mark_copy(r, row_peer(i)).wait_recv(), 2)
        column[...] = jnp.transpose(widen(jnp.sum(marks[...], axis=0)))
        loop(near, lambda i: mark_slot(c + i))

    def part_copy(k, peer, slot):
        return pltpu.make_async_remote_copy(
            src_ref=part_send.at[k, peer],
            dst_ref=part_recv.at[k, slot],
            send_sem=part_send_sem.at[peer],
            recv_sem=part_recv_sem.at[k, slot],
            device_id=target(r, peer),
            device_id_type=MESH,
        )

    def row_copy(k, peer, slot):
        return pltpu.make_async_remote_copy(
            src_ref=row_send.at[k],
            dst_ref=row_recv.at[k, slot],
            send_sem=row_send_sem.at[peer],
            recv_sem=row_recv_sem.at[k, slot],
            device_id=target(peer, c),
            device_id_type=MESH,
        )

    def all_copy(k, peer, slot):
        return pltpu.make_async_remote_copy(
            src_ref=all_send.at[k],
            dst_ref=all_recv.at[k, slot],
            send_sem=all_send_sem.at[peer],
            recv_sem=all_recv_sem.at[k, slot],
            device_id=target(r, peer),
            device_id_type=MESH,
        )

    def total(k, value, first_work, second_work, third_work):
        for p in range(cols):
            part_send[k, p] = value[p * group : (p + 1) * group, :]
        loop(cols, lambda i: part_copy(k, col_peer(i), c).start(), 1)
        part_recv[k, c] = part_send[k, c]
        first_work()
        loop(cols, lambda i: part_copy(k, c, col_peer(i)).wait_recv(), 1)
        row_part = jnp.sum(part_recv[k], axis=0)
        row_send[k] = row_part
        row_recv[k, r] = row_part
        loop(rows, lambda i: row_copy(k, row_peer(i), r).start(), 1)
        second_work()
        loop(rows, lambda i: row_copy(k, r, row_peer(i)).wait_recv(), 1)
        whole = jnp.sum(row_recv[k], axis=0)
        all_send[k] = whole
        all_recv[k, c] = whole
        loop(cols, lambda i: all_copy(k, col_peer(i), c).start(), 1)
        third_work()
        loop(cols, lambda i: all_copy(k, c, col_peer(i)).wait_recv(), 1)
        loop(cols, lambda i: part_copy(k, col_peer(i), c).wait_send(), 1)
        loop(rows, lambda i: row_copy(k, row_peer(i), r).wait_send(), 1)
        loop(cols, lambda i: all_copy(k, col_peer(i), c).wait_send(), 1)
        return jnp.concatenate([all_recv[k, p] for p in range(cols)], axis=0)

    def message(body, scalars):
        lane = lax.broadcasted_iota(jnp.int32, (outs, 128), 1)
        tail = jnp.zeros((outs, 128), F32)
        for index, scalar in enumerate(scalars):
            tail = jnp.where(lane == index, scalar, tail)
        return jnp.concatenate([body, tail], axis=1)

    def dots(first, second):
        return jnp.sum(first * second, axis=1, keepdims=True)

    def nothing():
        pass

    slots = cols + 2 * halo

    own_targets = data_in[c, PTS:, :]
    sums = total(
        0,
        message(
            product(own_targets, own_high[...], own_low[...]), [dots(own_targets, own_targets)]
        ),
        first_band,
        first_marks,
        nothing,
    )
    u0 = sums[:, :width]
    w0 = product(u0, core_high[...], core_low[...])
    rz0 = sums[:, width : width + 1] - dots(w0, u0)

    def apply_near(make):
        def step(i, running):
            slot = c + i
            place = r * cols + slot - halo
            valid = (place >= 0) & (place < rows * cols)
            value = jnp.where(valid, make(slot), 0.0)
            near_z[i] = value
            return running + product(value, band_high[i], band_low[i])

        image = lax.fori_loop(0, near, step, jnp.zeros((outs, width), F32))
        return image + ridge_shift * near_z[halo]

    def first_z(slot):
        return data[slot, PTS:, :] - product(w0, mark_high[slot], mark_low[slot])

    q0 = apply_near(first_z)
    z0_own = near_z[halo]
    q_send[0] = q0
    q_first[own] = q0

    def q_copy(index, row, col, slot):
        return pltpu.make_async_remote_copy(
            src_ref=q_send.at[0],
            dst_ref=q_first.at[slot],
            send_sem=q_send_sem.at[index],
            recv_sem=q_recv_sem.at[slot],
            device_id=target(row, col),
            device_id_type=MESH,
        )

    def send_index(peer):
        return 2 * halo + peer

    image_message = message(product(q0, own_high[...], own_low[...]), [dots(z0_own, q0)])

    def send_first():
        edge_peers(
            lambda index, row, col, slot: q_copy(
                index, row, col, jnp.where(row > r, c - cols + halo, halo + cols + c)
            ).start()
        )
        loop(cols, lambda i: q_copy(send_index(col_peer(i)), r, col_peer(i), own).start(), 1)
        loop(slots - near, lambda i: mark_slot(lax.rem(c + near + i, slots)))

    def first_slab(i):
        z_first[i] = first_z(halo + i)

    def take_first():
        edge_peers(lambda index, row, col, slot: q_copy(index, row, col, slot).wait_recv())
        loop(
            cols,
            lambda i: q_copy(send_index(c), r, c, halo + col_peer(i)).wait_recv(),
            1,
        )

    sums = total(
        1, image_message, send_first, lambda: loop(cols, first_slab), take_first
    )
    edge_peers(lambda index, row, col, slot: q_copy(index, row, col, slot).wait_send())
    loop(cols, lambda i: q_copy(send_index(col_peer(i)), r, col_peer(i), own).wait_send(), 1)

    curve0 = sums[:, width : width + 1]
    alpha0 = rz0 / curve0
    u1 = u0 - alpha0 * sums[:, :width]
    w1 = product(u1, core_high[...], core_low[...])

    def next_r(slot):
        return data[slot, PTS:, :] - alpha0 * q_first[slot]

    def next_z(slot):
        return next_r(slot) - product(w1, mark_high[slot], mark_low[slot])

    image = apply_near(next_z)
    z1_own = near_z[halo]
    r1_own = next_r(own)
    q_send[1] = image
    q_next[c] = image

    def q2_copy(peer, slot):
        return pltpu.make_async_remote_copy(
            src_ref=q_send.at[1],
            dst_ref=q_next.at[slot],
            send_sem=q2_send_sem.at[peer],
            recv_sem=q2_recv_sem.at[slot],
            device_id=target(r, peer),
            device_id_type=MESH,
        )

    def next_slab(i):
        residual = next_r(halo + i)
        r_next[i] = residual
        z_next[i] = residual - product(w1, mark_high[halo + i], mark_low[halo + i])

    lane = lax.broadcasted_iota(jnp.int32, (outs, 128), 1)
    line = lax.broadcasted_iota(jnp.int32, (outs, 128), 0)

    def small_copy(peer, slot):
        return pltpu.make_async_remote_copy(
            src_ref=small_send,
            dst_ref=small_recv.at[slot],
            send_sem=part_send_sem.at[peer],
            recv_sem=part_recv_sem.at[2, slot],
            device_id=target(r, peer),
            device_id_type=MESH,
        )

    def last_copy(peer, slot):
        return pltpu.make_async_remote_copy(
            src_ref=last_send,
            dst_ref=last_recv.at[slot],
            send_sem=row_send_sem.at[peer],
            recv_sem=row_recv_sem.at[2, slot],
            device_id=target(peer, c),
            device_id_type=MESH,
        )

    packed = jnp.zeros((outs, 128), F32)
    for index, scalar in enumerate(
        [dots(r1_own, z1_own), dots(z1_own, image), dots(z1_own, q0) + dots(z0_own, image)]
    ):
        packed = jnp.where(lane == line + index * outs, scalar, packed)
    packed = jnp.sum(packed, axis=0, keepdims=True)
    small_send[...] = packed
    small_recv[c] = packed
    loop(cols, lambda i: small_copy(col_peer(i), c).start(), 1)
    loop(cols, lambda i: q2_copy(col_peer(i), c).start(), 1)
    loop(cols // 2, next_slab)
    loop(cols, lambda i: small_copy(c, col_peer(i)).wait_recv(), 1)
    packed = jnp.sum(small_recv[...], axis=0)
    last_send[...] = packed
    last_recv[r] = packed
    loop(rows, lambda i: last_copy(row_peer(i), r).start(), 1)
    loop(cols, next_slab, cols // 2)
    loop(cols, lambda i: q2_copy(c, col_peer(i)).wait_recv(), 1)
    loop(rows, lambda i: last_copy(r, row_peer(i)).wait_recv(), 1)
    whole = jnp.sum(last_recv[...], axis=0)

    def taken(index):
        picked_lane = jnp.where(lane == line + index * outs, whole, 0.0)
        return jnp.sum(picked_lane, axis=1, keepdims=True)

    rz1 = taken(0)
    beta = rz1 / rz0
    curve1 = taken(1) + beta * (taken(2) + beta * curve0)
    alpha1 = rz1 / curve1

    def finish(i):
        at = pl.ds(pl.multiple_of(i * width, width), width)
        first = z_first[i]
        sol_out[:, at] = alpha0 * first + alpha1 * (z_next[i] + beta * first)
        res_out[:, at] = r_next[i] - alpha1 * (q_next[i] + beta * q_first[halo + i])

    loop(cols, finish)

    loop(cols, lambda i: small_copy(col_peer(i), c).wait_send(), 1)
    loop(rows, lambda i: last_copy(row_peer(i), r).wait_send(), 1)
    loop(cols, lambda i: q2_copy(col_peer(i), c).wait_send(), 1)
    loop(rows, lambda i: mark_copy(row_peer(i), r).wait_send(), 1)

    @pl.when(r < rows - 1)
    def _():
        halo_right().wait_send()

    @pl.when(r > 0)
    def _():
        halo_left().wait_send()


def body(points, targets, landmarks, neighbours, counts, core_inverse):
    cols = lax.axis_size("cols")
    rows = lax.axis_size("rows")
    row_index = lax.axis_index("rows")
    slab = points.shape[1]
    block = slab // neighbours.shape[0]
    width = slab // cols
    outs = targets.shape[0]
    land = landmarks.shape[0]
    halo = -(-REACH * block // width)
    near = 2 * halo + 1
    slots = cols + 2 * halo

    local_ids = landmarks - row_index * slab
    present = (local_ids >= 0) & (local_ids < slab)
    picked = jnp.take(points, jnp.clip(local_ids, 0, slab - 1), axis=1)
    picked = jnp.where(present[None, :], picked, 0.0)
    picked = jnp.concatenate([picked, jnp.zeros((1, land), F32)], axis=0)
    close = (local_ids >= -slab) & (local_ids < 2 * slab)
    close = jnp.broadcast_to(close[None, :].astype(F32), (8, land))
    lines = PTS + outs
    data = jnp.concatenate([points, jnp.zeros((PTS - 3, slab), F32), targets], axis=0)
    data = data.reshape(lines, cols, width).transpose(1, 0, 2)

    vmem = pltpu.VMEM
    dma = pltpu.SemaphoreType.DMA
    group = outs // cols
    wide = land + 128
    scratch = [
        vmem((slots, lines, width), F32),
        vmem((rows, 4, land), F32),
        vmem((width, PTS), F32),
        vmem((near, width, width), BF16),
        vmem((near, width, width), BF16),
        vmem((slots, land, width), BF16),
        vmem((slots, land, width), BF16),
        vmem((width, land), BF16),
        vmem((width, land), BF16),
        vmem((land, land), BF16),
        vmem((land, land), BF16),
        vmem((near, outs, width), F32),
        vmem((cols, outs, width), F32),
        vmem((cols, outs, width), F32),
        vmem((cols, outs, width), F32),
        vmem((2, outs, width), F32),
        vmem((slots, outs, width), F32),
        vmem((cols, outs, width), F32),
        vmem((2, cols, group, wide), F32),
        vmem((2, cols, group, wide), F32),
        vmem((2, group, wide), F32),
        vmem((2, rows, group, wide), F32),
        vmem((2, group, wide), F32),
        vmem((2, cols, group, wide), F32),
        vmem((1, 128), F32),
        vmem((cols, 1, 128), F32),
        vmem((1, 128), F32),
        vmem((rows, 1, 128), F32),
        dma((2,)),
        dma((2,)),
        dma((rows,)),
        dma((rows,)),
        dma((slots,)),
        dma((slots,)),
        dma((cols,)),
        dma((cols,)),
        dma((cols,)),
        dma((3, cols)),
        dma((rows,)),
        dma((3, rows)),
        dma((cols,)),
        dma((2, cols)),
    ]
    shape = jax.ShapeDtypeStruct((outs, slab), F32)
    return tuple(
        pl.pallas_call(
            functools.partial(solve_kernel, rows, cols, halo),
            out_shape=(shape, shape),
            in_specs=[pl.BlockSpec(memory_space=pltpu.VMEM)] * 4,
            out_specs=[pl.BlockSpec(memory_space=pltpu.VMEM)] * 2,
            scratch_shapes=scratch,
            compiler_params=pltpu.CompilerParams(
                collective_id=0,
                has_side_effects=True,
                vmem_limit_bytes=48 * 1024 * 1024,
            ),
        )(data, picked, close, core_inverse)
    )


def solution(mesh):
    placed = (P(None, "rows"), P(None, "rows"), P(), P("rows", None), P("rows"), P())
    return jax.shard_map(
        body,
        mesh=mesh,
        in_specs=placed,
        out_specs=(P(None, "rows"), P(None, "rows")),
        check_vma=False,
    )
```

```python
import functools

import jax
import jax.numpy as jnp
from jax import lax
from jax.experimental import pallas as pl
from jax.experimental.pallas import tpu as pltpu
from jax.sharding import PartitionSpec as P

MOST = 6
REACH = 2 * MOST

kernel_scale = 0.03125
ridge_shift = 1.0

F32 = jnp.float32
BF16 = jnp.bfloat16
MESH = pl.DeviceIdType.MESH
PTS = 8


def halves(value):
    high = value.astype(BF16)
    return high, (value - high.astype(F32)).astype(BF16)


def product(value, high, low):
    rows = value.shape[0]
    value_high, value_low = halves(value)
    both = jnp.concatenate([value_high, value_low], axis=0)
    first = jnp.dot(both, high, preferred_element_type=F32)
    second = jnp.dot(value_high, low, preferred_element_type=F32)
    return first[:rows] + (first[rows:] + second)


def kernel_rows(column, lanes):
    squared = None
    for dim in range(3):
        offsets = column[:, dim : dim + 1] - lanes[dim : dim + 1, :]
        term = offsets * offsets
        squared = term if squared is None else squared + term
    distance = squared * lax.rsqrt(jnp.maximum(squared, 1e-30))
    remain = jnp.maximum(1.0 - distance, 0.0)
    square = remain * remain
    return (square * square) * ((4.0 * kernel_scale) * distance + kernel_scale)


def solve_kernel(
    rows,
    cols,
    halo,
    data_in,
    picked,
    close,
    core,
    sol_out,
    res_out,
    data,
    marks,
    column,
    band_high,
    band_low,
    mark_high,
    mark_low,
    own_high,
    own_low,
    core_high,
    core_low,
    near_z,
    z_first,
    z_next,
    r_next,
    q_send,
    q_first,
    q_next,
    part_send,
    part_recv,
    row_send,
    row_recv,
    all_send,
    all_recv,
    small_send,
    small_recv,
    last_send,
    last_recv,
    halo_send_sem,
    halo_recv_sem,
    mark_send_sem,
    mark_recv_sem,
    q_send_sem,
    q_recv_sem,
    q2_send_sem,
    q2_recv_sem,
    part_send_sem,
    part_recv_sem,
    row_send_sem,
    row_recv_sem,
    all_send_sem,
    all_recv_sem,
):
    r = lax.axis_index("rows")
    c = lax.axis_index("cols")
    width = data.shape[2]
    outs = data.shape[1] - PTS
    near = 2 * halo + 1
    piece = 64
    group = outs // cols

    def target(row, col):
        return (row, col)

    def col_peer(step):
        return lax.rem(c + step, cols)

    def row_peer(step):
        return lax.rem(r + step, rows)

    def loop(count, fn, start=0):
        def step(i, carry):
            fn(i)
            return carry

        lax.fori_loop(start, count, step, 0)

    def edge_peers(fn):
        def one(k):
            @pl.when((r < rows - 1) & (k <= c + halo - cols))
            def _():
                fn(k, r + 1, k, halo + cols + k)

            @pl.when((r > 0) & (k >= c))
            def _():
                fn(halo + k, r - 1, cols - halo + k, k)

        loop(halo, one)

    def bulk(ref, send_sem, recv_sem):
        return pltpu.make_async_remote_copy(
            src_ref=ref,
            dst_ref=ref,
            send_sem=send_sem,
            recv_sem=recv_sem,
            device_id=target(r, c),
            device_id_type=MESH,
        )

    barrier = pltpu.get_barrier_semaphore()

    def greet(row, col):
        pl.semaphore_signal(barrier, inc=1, device_id=target(row, col), device_id_type=MESH)

    loop(cols, lambda i: greet(r, col_peer(i)), 1)
    loop(rows, lambda i: greet(row_peer(i), c), 1)
    edge_peers(lambda index, row, col, slot: greet(row, col))
    right_extra = jnp.where(r < rows - 1, jnp.maximum(c + halo - cols + 1, 0), 0)
    left_extra = jnp.where(r > 0, jnp.maximum(halo - c, 0), 0)
    pl.semaphore_wait(barrier, cols + rows - 2 + right_extra + left_extra)

    def halo_right():
        return pltpu.make_async_remote_copy(
            src_ref=data_in.at[pl.ds(cols - halo, halo)],
            dst_ref=data.at[pl.ds(0, halo)],
            send_sem=halo_send_sem.at[0],
            recv_sem=halo_recv_sem.at[0],
            device_id=target(jnp.minimum(r + 1, rows - 1), c),
            device_id_type=MESH,
        )

    def halo_left():
        return pltpu.make_async_remote_copy(
            src_ref=data_in.at[pl.ds(0, halo)],
            dst_ref=data.at[pl.ds(halo + cols, halo)],
            send_sem=halo_send_sem.at[1],
            recv_sem=halo_recv_sem.at[1],
            device_id=target(jnp.maximum(r - 1, 0), c),
            device_id_type=MESH,
        )

    def mark_copy(peer, slot, sem=2):
        return pltpu.make_async_remote_copy(
            src_ref=picked,
            dst_ref=marks.at[slot],
            send_sem=mark_send_sem.at[sem],
            recv_sem=mark_recv_sem.at[sem],
            device_id=target(peer, c),
            device_id_type=MESH,
        )

    mark_copy(row_peer(1), r, 0).start()
    mark_copy(row_peer(rows - 1), r, 1).start()
    loop(rows - 1, lambda i: mark_copy(row_peer(i), r).start(), 2)

    @pl.when(r < rows - 1)
    def _():
        halo_right().start()

    @pl.when(r > 0)
    def _():
        halo_left().start()

    def keep(i):
        data[halo + i] = data_in[i]

    loop(cols, keep)
    marks[r] = picked[...]
    high, low = halves(core[...])
    core_high[...] = high
    core_low[...] = low

    @pl.when(r == 0)
    def _():
        data[0:halo] = jnp.zeros((halo,) + data.shape[1:], F32)

    @pl.when(r == rows - 1)
    def _():
        data[halo + cols : 2 * halo + cols] = jnp.zeros((halo,) + data.shape[1:], F32)

    own = c + halo

    def fill(lanes, put):
        def one(i):
            at = pl.multiple_of(i * piece, piece)
            high, low = halves(kernel_rows(column[pl.ds(at, piece), :], lanes))
            put(at, high, low)

        for i in range(width // piece):
            one(i)

    own_lanes = data_in[c, 0:PTS, :]

    def band_slot(i):
        column[...] = jnp.transpose(data[c + i, 0:PTS, :])

        def put(at, high, low):
            band_high[i, pl.ds(at, piece), :] = high
            band_low[i, pl.ds(at, piece), :] = low

        fill(own_lanes, put)

    def widen(lanes):
        return jnp.concatenate([lanes, jnp.zeros((PTS - lanes.shape[0], width), F32)], axis=0)

    before = row_peer(rows - 1)
    after = row_peer(1)
    mark_copy(r, before, 0).wait_recv()
    mark_copy(r, after, 1).wait_recv()
    close_lanes = widen(marks[before] + picked[...] + marks[after])
    column[...] = jnp.transpose(own_lanes)
    close_row = close[0:1, :]

    def put_own(at, high, low):
        high = high * close_row.astype(BF16)
        low = low * close_row.astype(BF16)
        own_high[pl.ds(at, piece), :] = high
        own_low[pl.ds(at, piece), :] = low

    fill(close_lanes, put_own)

    def mark_slot(i):
        def put(at, high, low):
            mark_high[i, pl.ds(at, piece), :] = high
            mark_low[i, pl.ds(at, piece), :] = low

        fill(data[i, 0:PTS, :], put)

    def first_band():
        @pl.when(r > 0)
        def _():
            halo_right().wait_recv()

        @pl.when(r < rows - 1)
        def _():
            halo_left().wait_recv()

        loop(near, band_slot)

    def marks_done():
        return bulk(marks.at[pl.ds(0, rows - 3)], mark_send_sem.at[2], mark_recv_sem.at[2])

    def first_marks():
        marks_done().wait_recv()
        column[...] = jnp.transpose(widen(jnp.sum(marks[...], axis=0)))
        loop(near, lambda i: mark_slot(c + i))

    def part_copy(k, peer, slot):
        return pltpu.make_async_remote_copy(
            src_ref=part_send.at[k, peer],
            dst_ref=part_recv.at[k, slot],
            send_sem=part_send_sem.at[k],
            recv_sem=part_recv_sem.at[k],
            device_id=target(r, peer),
            device_id_type=MESH,
        )

    def row_copy(k, peer, slot):
        return pltpu.make_async_remote_copy(
            src_ref=row_send.at[k],
            dst_ref=row_recv.at[k, slot],
            send_sem=row_send_sem.at[k],
            recv_sem=row_recv_sem.at[k],
            device_id=target(peer, c),
            device_id_type=MESH,
        )

    def all_copy(k, peer, slot):
        return pltpu.make_async_remote_copy(
            src_ref=all_send.at[k],
            dst_ref=all_recv.at[k, slot],
            send_sem=all_send_sem.at[k],
            recv_sem=all_recv_sem.at[k],
            device_id=target(r, peer),
            device_id_type=MESH,
        )

    def part_done(k):
        return bulk(part_recv.at[k, pl.ds(0, cols - 1)], part_send_sem.at[k], part_recv_sem.at[k])

    def row_done(k):
        return bulk(row_recv.at[k, pl.ds(0, rows - 1)], row_send_sem.at[k], row_recv_sem.at[k])

    def all_done(k):
        return bulk(all_recv.at[k, pl.ds(0, cols - 1)], all_send_sem.at[k], all_recv_sem.at[k])

    def total(k, value, first_work, second_work, third_work):
        for p in range(cols):
            part_send[k, p] = value[p * group : (p + 1) * group, :]
        loop(cols, lambda i: part_copy(k, col_peer(i), c).start(), 1)
        part_recv[k, c] = part_send[k, c]
        first_work()
        part_done(k).wait_recv()
        row_part = jnp.sum(part_recv[k], axis=0)
        row_send[k] = row_part
        row_recv[k, r] = row_part
        loop(rows, lambda i: row_copy(k, row_peer(i), r).start(), 1)
        second_work()
        row_done(k).wait_recv()
        whole = jnp.sum(row_recv[k], axis=0)
        all_send[k] = whole
        all_recv[k, c] = whole
        loop(cols, lambda i: all_copy(k, col_peer(i), c).start(), 1)
        third_work()
        all_done(k).wait_recv()
        return jnp.concatenate([all_recv[k, p] for p in range(cols)], axis=0)

    def message(body, scalars):
        lane = lax.broadcasted_iota(jnp.int32, (outs, 128), 1)
        tail = jnp.zeros((outs, 128), F32)
        for index, scalar in enumerate(scalars):
            tail = jnp.where(lane == index, scalar, tail)
        return jnp.concatenate([body, tail], axis=1)

    def dots(first, second):
        return jnp.sum(first * second, axis=1, keepdims=True)

    def nothing():
        pass

    slots = cols + 2 * halo

    own_targets = data_in[c, PTS:, :]
    sums = total(
        0,
        message(
            product(own_targets, own_high[...], own_low[...]), [dots(own_targets, own_targets)]
        ),
        first_band,
        first_marks,
        nothing,
    )
    u0 = sums[:, :width]
    w0 = product(u0, core_high[...], core_low[...])
    rz0 = sums[:, width : width + 1] - dots(w0, u0)

    def apply_near(make):
        def step(i, running):
            slot = c + i
            place = r * cols + slot - halo
            valid = (place >= 0) & (place < rows * cols)
            value = jnp.where(valid, make(slot), 0.0)
            near_z[i] = value
            return running + product(value, band_high[i], band_low[i])

        image = lax.fori_loop(0, near, step, jnp.zeros((outs, width), F32))
        return image + ridge_shift * near_z[halo]

    def first_z(slot):
        return data[slot, PTS:, :] - product(w0, mark_high[slot], mark_low[slot])

    q0 = apply_near(first_z)
    z0_own = near_z[halo]
    q_send[0] = q0
    q_first[own] = q0

    def q_copy(index, row, col, slot, sem=None):
        return pltpu.make_async_remote_copy(
            src_ref=q_send.at[0],
            dst_ref=q_first.at[slot],
            send_sem=q_send_sem.at[index],
            recv_sem=q_recv_sem.at[slot if sem is None else sem],
            device_id=target(row, col),
            device_id_type=MESH,
        )

    def q_done():
        return bulk(q_first.at[pl.ds(0, cols - 1)], q_send_sem.at[slots], q_recv_sem.at[slots])

    image_message = message(product(q0, own_high[...], own_low[...]), [dots(z0_own, q0)])

    def send_first():
        edge_peers(
            lambda index, row, col, slot: q_copy(
                index, row, col, jnp.where(row > r, c - cols + halo, halo + cols + c)
            ).start()
        )
        loop(cols, lambda i: q_copy(slots, r, col_peer(i), own, slots).start(), 1)
        loop(slots - near, lambda i: mark_slot(lax.rem(c + near + i, slots)))

    def first_slab(i):
        z_first[i] = first_z(halo + i)

    def take_first():
        edge_peers(lambda index, row, col, slot: q_copy(index, row, col, slot).wait_recv())
        q_done().wait_recv()

    sums = total(
        1, image_message, send_first, lambda: loop(cols, first_slab), take_first
    )

    curve0 = sums[:, width : width + 1]
    alpha0 = rz0 / curve0
    u1 = u0 - alpha0 * sums[:, :width]
    w1 = product(u1, core_high[...], core_low[...])

    def next_r(slot):
        return data[slot, PTS:, :] - alpha0 * q_first[slot]

    def next_z(slot):
        return next_r(slot) - product(w1, mark_high[slot], mark_low[slot])

    image = apply_near(next_z)
    z1_own = near_z[halo]
    r1_own = next_r(own)
    q_send[1] = image
    q_next[c] = image

    def q2_copy(peer, slot):
        return pltpu.make_async_remote_copy(
            src_ref=q_send.at[1],
            dst_ref=q_next.at[slot],
            send_sem=q2_send_sem.at[0],
            recv_sem=q2_recv_sem.at[0],
            device_id=target(r, peer),
            device_id_type=MESH,
        )

    def next_slab(i):
        residual = next_r(halo + i)
        r_next[i] = residual
        z_next[i] = residual - product(w1, mark_high[halo + i], mark_low[halo + i])

    lane = lax.broadcasted_iota(jnp.int32, (outs, 128), 1)
    line = lax.broadcasted_iota(jnp.int32, (outs, 128), 0)

    def small_copy(peer, slot):
        return pltpu.make_async_remote_copy(
            src_ref=small_send,
            dst_ref=small_recv.at[slot],
            send_sem=part_send_sem.at[2],
            recv_sem=part_recv_sem.at[2],
            device_id=target(r, peer),
            device_id_type=MESH,
        )

    def last_copy(peer, slot):
        return pltpu.make_async_remote_copy(
            src_ref=last_send,
            dst_ref=last_recv.at[slot],
            send_sem=row_send_sem.at[2],
            recv_sem=row_recv_sem.at[2],
            device_id=target(peer, c),
            device_id_type=MESH,
        )

    packed = jnp.zeros((outs, 128), F32)
    for index, scalar in enumerate(
        [dots(r1_own, z1_own), dots(z1_own, image), dots(z1_own, q0) + dots(z0_own, image)]
    ):
        packed = jnp.where(lane == line + index * outs, scalar, packed)
    packed = jnp.sum(packed, axis=0, keepdims=True)
    small_send[...] = packed
    small_recv[c] = packed
    loop(cols, lambda i: small_copy(col_peer(i), c).start(), 1)
    loop(cols, lambda i: q2_copy(col_peer(i), c).start(), 1)
    loop(cols // 2, next_slab)
    small_done = bulk(
        small_recv.at[pl.ds(0, cols - 1)], part_send_sem.at[2], part_recv_sem.at[2]
    )
    small_done.wait_recv()
    packed = jnp.sum(small_recv[...], axis=0)
    last_send[...] = packed
    last_recv[r] = packed
    loop(rows, lambda i: last_copy(row_peer(i), r).start(), 1)
    loop(cols, next_slab, cols // 2)
    q2_done = bulk(q_next.at[pl.ds(0, cols - 1)], q2_send_sem.at[0], q2_recv_sem.at[0])
    q2_done.wait_recv()
    last_done = bulk(last_recv.at[pl.ds(0, rows - 1)], row_send_sem.at[2], row_recv_sem.at[2])
    last_done.wait_recv()
    whole = jnp.sum(last_recv[...], axis=0)

    def taken(index):
        picked_lane = jnp.where(lane == line + index * outs, whole, 0.0)
        return jnp.sum(picked_lane, axis=1, keepdims=True)

    rz1 = taken(0)
    beta = rz1 / rz0
    curve1 = taken(1) + beta * (taken(2) + beta * curve0)
    alpha1 = rz1 / curve1

    def finish(i):
        at = pl.ds(pl.multiple_of(i * width, width), width)
        first = z_first[i]
        sol_out[:, at] = alpha0 * first + alpha1 * (z_next[i] + beta * first)
        res_out[:, at] = r_next[i] - alpha1 * (q_next[i] + beta * q_first[halo + i])

    loop(cols, finish)

    for k in range(2):
        part_done(k).wait_send()
        row_done(k).wait_send()
        all_done(k).wait_send()
    small_done.wait_send()
    last_done.wait_send()
    edge_peers(lambda index, row, col, slot: q_copy(index, row, col, slot).wait_send())
    q_done().wait_send()
    q2_done.wait_send()
    mark_copy(row_peer(1), r, 0).wait_send()
    mark_copy(row_peer(rows - 1), r, 1).wait_send()
    marks_done().wait_send()

    @pl.when(r < rows - 1)
    def _():
        halo_right().wait_send()

    @pl.when(r > 0)
    def _():
        halo_left().wait_send()


def body(points, targets, landmarks, neighbours, counts, core_inverse):
    cols = lax.axis_size("cols")
    rows = lax.axis_size("rows")
    row_index = lax.axis_index("rows")
    slab = points.shape[1]
    block = slab // neighbours.shape[0]
    width = slab // cols
    outs = targets.shape[0]
    land = landmarks.shape[0]
    halo = -(-REACH * block // width)
    near = 2 * halo + 1
    slots = cols + 2 * halo

    local_ids = landmarks - row_index * slab
    present = (local_ids >= 0) & (local_ids < slab)
    picked = jnp.take(points, jnp.clip(local_ids, 0, slab - 1), axis=1)
    picked = jnp.where(present[None, :], picked, 0.0)
    picked = jnp.concatenate([picked, jnp.zeros((1, land), F32)], axis=0)
    close = (local_ids >= -slab) & (local_ids < 2 * slab)
    close = jnp.broadcast_to(close[None, :].astype(F32), (8, land))
    lines = PTS + outs
    data = jnp.concatenate([points, jnp.zeros((PTS - 3, slab), F32), targets], axis=0)
    data = data.reshape(lines, cols, width).transpose(1, 0, 2)

    vmem = pltpu.VMEM
    dma = pltpu.SemaphoreType.DMA
    group = outs // cols
    wide = land + 128
    scratch = [
        vmem((slots, lines, width), F32),
        vmem((rows, 4, land), F32),
        vmem((width, PTS), F32),
        vmem((near, width, width), BF16),
        vmem((near, width, width), BF16),
        vmem((slots, land, width), BF16),
        vmem((slots, land, width), BF16),
        vmem((width, land), BF16),
        vmem((width, land), BF16),
        vmem((land, land), BF16),
        vmem((land, land), BF16),
        vmem((near, outs, width), F32),
        vmem((cols, outs, width), F32),
        vmem((cols, outs, width), F32),
        vmem((cols, outs, width), F32),
        vmem((2, outs, width), F32),
        vmem((slots, outs, width), F32),
        vmem((cols, outs, width), F32),
        vmem((2, cols, group, wide), F32),
        vmem((2, cols, group, wide), F32),
        vmem((2, group, wide), F32),
        vmem((2, rows, group, wide), F32),
        vmem((2, group, wide), F32),
        vmem((2, cols, group, wide), F32),
        vmem((1, 128), F32),
        vmem((cols, 1, 128), F32),
        vmem((1, 128), F32),
        vmem((rows, 1, 128), F32),
        dma((2,)),
        dma((2,)),
        dma((3,)),
        dma((3,)),
        dma((slots + 1,)),
        dma((slots + 1,)),
        dma((1,)),
        dma((1,)),
        dma((3,)),
        dma((3,)),
        dma((3,)),
        dma((3,)),
        dma((2,)),
        dma((2,)),
    ]
    shape = jax.ShapeDtypeStruct((outs, slab), F32)
    return tuple(
        pl.pallas_call(
            functools.partial(solve_kernel, rows, cols, halo),
            out_shape=(shape, shape),
            in_specs=[pl.BlockSpec(memory_space=pltpu.VMEM)] * 4,
            out_specs=[pl.BlockSpec(memory_space=pltpu.VMEM)] * 2,
            scratch_shapes=scratch,
            compiler_params=pltpu.CompilerParams(
                collective_id=0,
                has_side_effects=True,
                vmem_limit_bytes=48 * 1024 * 1024,
            ),
        )(data, picked, close, core_inverse)
    )


def solution(mesh):
    placed = (P(None, "rows"), P(None, "rows"), P(), P("rows", None), P("rows"), P())
    return jax.shard_map(
        body,
        mesh=mesh,
        in_specs=placed,
        out_specs=(P(None, "rows"), P(None, "rows")),
        check_vma=False,
    )
```

```python
import functools

import jax
import jax.numpy as jnp
from jax import lax
from jax.experimental import pallas as pl
from jax.experimental.pallas import tpu as pltpu
from jax.sharding import PartitionSpec as P

MOST = 6
REACH = 2 * MOST

kernel_scale = 0.03125
ridge_shift = 1.0

F32 = jnp.float32
BF16 = jnp.bfloat16
MESH = pl.DeviceIdType.MESH
PTS = 8


def halves(value):
    high = value.astype(BF16)
    return high, (value - high.astype(F32)).astype(BF16)


def product(value, high, low):
    rows = value.shape[0]
    value_high, value_low = halves(value)
    both = jnp.concatenate([value_high, value_low], axis=0)
    first = jnp.dot(both, high, preferred_element_type=F32)
    second = jnp.dot(value_high, low, preferred_element_type=F32)
    return first[:rows] + (first[rows:] + second)


def kernel_rows(column, lanes):
    squared = None
    for dim in range(3):
        offsets = column[:, dim : dim + 1] - lanes[dim : dim + 1, :]
        term = offsets * offsets
        squared = term if squared is None else squared + term
    distance = squared * lax.rsqrt(jnp.maximum(squared, 1e-30))
    remain = jnp.maximum(1.0 - distance, 0.0)
    square = remain * remain
    return (square * square) * ((4.0 * kernel_scale) * distance + kernel_scale)


def solve_kernel(
    rows,
    cols,
    halo,
    data_in,
    picked,
    close,
    core,
    sol_out,
    res_out,
    data,
    marks,
    column,
    band_high,
    band_low,
    mark_high,
    mark_low,
    own_high,
    own_low,
    core_high,
    core_low,
    near_z,
    z_first,
    z_next,
    r_next,
    q_send,
    q_first,
    q_next,
    part_send,
    part_recv,
    row_send,
    row_recv,
    all_send,
    all_recv,
    small_send,
    small_recv,
    last_send,
    last_recv,
    halo_send_sem,
    halo_recv_sem,
    mark_send_sem,
    mark_recv_sem,
    q_send_sem,
    q_recv_sem,
    q2_send_sem,
    q2_recv_sem,
    part_send_sem,
    part_recv_sem,
    row_send_sem,
    row_recv_sem,
    all_send_sem,
    all_recv_sem,
):
    r = lax.axis_index("rows")
    c = lax.axis_index("cols")
    width = data.shape[2]
    outs = data.shape[1] - PTS
    near = 2 * halo + 1
    piece = 64
    group = outs // cols

    def target(row, col):
        return (row, col)

    def col_peer(step):
        return lax.rem(c + step, cols)

    def row_peer(step):
        return lax.rem(r + step, rows)

    def loop(count, fn, start=0):
        def step(i, carry):
            fn(i)
            return carry

        lax.fori_loop(start, count, step, 0)

    def edge_peers(fn):
        def one(k):
            @pl.when((r < rows - 1) & (k <= c + halo - cols))
            def _():
                fn(k, r + 1, k, halo + cols + k)

            @pl.when((r > 0) & (k >= c))
            def _():
                fn(halo + k, r - 1, cols - halo + k, k)

        loop(halo, one)

    def bulk(ref, send_sem, recv_sem):
        return pltpu.make_async_remote_copy(
            src_ref=ref,
            dst_ref=ref,
            send_sem=send_sem,
            recv_sem=recv_sem,
            device_id=target(r, c),
            device_id_type=MESH,
        )

    barrier = pltpu.get_barrier_semaphore()

    def greet(row, col):
        pl.semaphore_signal(barrier, inc=1, device_id=target(row, col), device_id_type=MESH)

    loop(cols, lambda i: greet(r, col_peer(i)), 1)
    loop(rows, lambda i: greet(row_peer(i), c), 1)
    edge_peers(lambda index, row, col, slot: greet(row, col))
    right_extra = jnp.where(r < rows - 1, jnp.maximum(c + halo - cols + 1, 0), 0)
    left_extra = jnp.where(r > 0, jnp.maximum(halo - c, 0), 0)
    pl.semaphore_wait(barrier, cols + rows - 2 + right_extra + left_extra)

    def halo_right():
        return pltpu.make_async_remote_copy(
            src_ref=data_in.at[pl.ds(cols - halo, halo)],
            dst_ref=data.at[pl.ds(0, halo)],
            send_sem=halo_send_sem.at[0],
            recv_sem=halo_recv_sem.at[0],
            device_id=target(jnp.minimum(r + 1, rows - 1), c),
            device_id_type=MESH,
        )

    def halo_left():
        return pltpu.make_async_remote_copy(
            src_ref=data_in.at[pl.ds(0, halo)],
            dst_ref=data.at[pl.ds(halo + cols, halo)],
            send_sem=halo_send_sem.at[1],
            recv_sem=halo_recv_sem.at[1],
            device_id=target(jnp.maximum(r - 1, 0), c),
            device_id_type=MESH,
        )

    def mark_copy(peer, slot, sem=2):
        return pltpu.make_async_remote_copy(
            src_ref=picked,
            dst_ref=marks.at[slot],
            send_sem=mark_send_sem.at[sem],
            recv_sem=mark_recv_sem.at[sem],
            device_id=target(peer, c),
            device_id_type=MESH,
        )

    mark_copy(row_peer(1), r, 0).start()
    mark_copy(row_peer(rows - 1), r, 1).start()
    loop(rows - 1, lambda i: mark_copy(row_peer(i), r).start(), 2)

    @pl.when(r < rows - 1)
    def _():
        halo_right().start()

    @pl.when(r > 0)
    def _():
        halo_left().start()

    def keep(i):
        data[halo + i] = data_in[i]

    loop(cols, keep)
    marks[r] = picked[...]
    high, low = halves(core[...])
    core_high[...] = high
    core_low[...] = low

    @pl.when(r == 0)
    def _():
        data[0:halo] = jnp.zeros((halo,) + data.shape[1:], F32)

    @pl.when(r == rows - 1)
    def _():
        data[halo + cols : 2 * halo + cols] = jnp.zeros((halo,) + data.shape[1:], F32)

    own = c + halo

    def fill(lanes, put):
        def one(i):
            at = pl.multiple_of(i * piece, piece)
            high, low = halves(kernel_rows(column[pl.ds(at, piece), :], lanes))
            put(at, high, low)

        for i in range(width // piece):
            one(i)

    own_lanes = data_in[c, 0:PTS, :]

    def band_slot(i):
        column[...] = jnp.transpose(data[c + i, 0:PTS, :])

        def put(at, high, low):
            band_high[i, pl.ds(at, piece), :] = high
            band_low[i, pl.ds(at, piece), :] = low

        fill(own_lanes, put)

    def widen(lanes):
        return jnp.concatenate([lanes, jnp.zeros((PTS - lanes.shape[0], width), F32)], axis=0)

    before = row_peer(rows - 1)
    after = row_peer(1)
    mark_copy(r, before, 0).wait_recv()
    mark_copy(r, after, 1).wait_recv()
    close_lanes = widen(marks[before] + picked[...] + marks[after])
    column[...] = jnp.transpose(own_lanes)
    close_row = close[0:1, :]

    def put_own(at, high, low):
        high = high * close_row.astype(BF16)
        low = low * close_row.astype(BF16)
        own_high[pl.ds(at, piece), :] = high
        own_low[pl.ds(at, piece), :] = low

    fill(close_lanes, put_own)

    def mark_slot(i):
        def put(at, high, low):
            mark_high[i, pl.ds(at, piece), :] = high
            mark_low[i, pl.ds(at, piece), :] = low

        fill(data[i, 0:PTS, :], put)

    def first_band():
        @pl.when(r > 0)
        def _():
            halo_right().wait_recv()

        @pl.when(r < rows - 1)
        def _():
            halo_left().wait_recv()

        loop(near, band_slot)

    def marks_done():
        return bulk(marks.at[pl.ds(0, rows - 3)], mark_send_sem.at[2], mark_recv_sem.at[2])

    def first_marks():
        marks_done().wait_recv()
        column[...] = jnp.transpose(widen(jnp.sum(marks[...], axis=0)))
        loop(near, lambda i: mark_slot(c + i))

    def part_copy(k, peer, slot):
        return pltpu.make_async_remote_copy(
            src_ref=part_send.at[k, peer],
            dst_ref=part_recv.at[k, slot],
            send_sem=part_send_sem.at[k],
            recv_sem=part_recv_sem.at[k],
            device_id=target(r, peer),
            device_id_type=MESH,
        )

    def row_copy(k, peer, slot):
        return pltpu.make_async_remote_copy(
            src_ref=row_send.at[k],
            dst_ref=row_recv.at[k, slot],
            send_sem=row_send_sem.at[k],
            recv_sem=row_recv_sem.at[k],
            device_id=target(peer, c),
            device_id_type=MESH,
        )

    def all_copy(k, peer, slot):
        return pltpu.make_async_remote_copy(
            src_ref=all_send.at[k],
            dst_ref=all_recv.at[k, slot],
            send_sem=all_send_sem.at[k],
            recv_sem=all_recv_sem.at[k],
            device_id=target(r, peer),
            device_id_type=MESH,
        )

    def part_done(k):
        return bulk(part_recv.at[k, pl.ds(0, cols - 1)], part_send_sem.at[k], part_recv_sem.at[k])

    def row_done(k):
        return bulk(row_recv.at[k, pl.ds(0, rows - 1)], row_send_sem.at[k], row_recv_sem.at[k])

    def all_done(k):
        return bulk(all_recv.at[k, pl.ds(0, cols - 1)], all_send_sem.at[k], all_recv_sem.at[k])

    def total(k, value, first_work, second_work, third_work):
        for p in range(cols):
            part_send[k, p] = value[p * group : (p + 1) * group, :]
        loop(cols, lambda i: part_copy(k, col_peer(i), c).start(), 1)
        part_recv[k, c] = part_send[k, c]
        first_work()
        part_done(k).wait_recv()
        row_part = jnp.sum(part_recv[k], axis=0)
        row_send[k] = row_part
        row_recv[k, r] = row_part
        loop(rows, lambda i: row_copy(k, row_peer(i), r).start(), 1)
        second_work()
        row_done(k).wait_recv()
        whole = jnp.sum(row_recv[k], axis=0)
        all_send[k] = whole
        all_recv[k, c] = whole
        loop(cols, lambda i: all_copy(k, col_peer(i), c).start(), 1)
        third_work()
        all_done(k).wait_recv()
        return jnp.concatenate([all_recv[k, p] for p in range(cols)], axis=0)

    def message(body, scalars):
        lane = lax.broadcasted_iota(jnp.int32, (outs, 128), 1)
        tail = jnp.zeros((outs, 128), F32)
        for index, scalar in enumerate(scalars):
            tail = jnp.where(lane == index, scalar, tail)
        return jnp.concatenate([body, tail], axis=1)

    def dots(first, second):
        return jnp.sum(first * second, axis=1, keepdims=True)

    def nothing():
        pass

    slots = cols + 2 * halo

    own_targets = data_in[c, PTS:, :]
    sums = total(
        0,
        message(
            product(own_targets, own_high[...], own_low[...]), [dots(own_targets, own_targets)]
        ),
        first_band,
        first_marks,
        nothing,
    )
    u0 = sums[:, :width]
    w0 = product(u0, core_high[...], core_low[...])
    rz0 = sums[:, width : width + 1] - dots(w0, u0)

    def apply_near(make):
        def step(i, running):
            slot = c + i
            place = r * cols + slot - halo
            valid = (place >= 0) & (place < rows * cols)
            value = jnp.where(valid, make(slot), 0.0)
            near_z[i] = value
            return running + product(value, band_high[i], band_low[i])

        image = lax.fori_loop(0, near, step, jnp.zeros((outs, width), F32))
        return image + ridge_shift * near_z[halo]

    def first_z(slot):
        return data[slot, PTS:, :] - product(w0, mark_high[slot], mark_low[slot])

    q0 = apply_near(first_z)
    z0_own = near_z[halo]
    q_send[0] = q0
    q_first[own] = q0

    def q_copy(index, row, col, slot, sem=None):
        return pltpu.make_async_remote_copy(
            src_ref=q_send.at[0],
            dst_ref=q_first.at[slot],
            send_sem=q_send_sem.at[index],
            recv_sem=q_recv_sem.at[slot if sem is None else sem],
            device_id=target(row, col),
            device_id_type=MESH,
        )

    def q_done():
        return bulk(q_first.at[pl.ds(0, cols - 1)], q_send_sem.at[slots], q_recv_sem.at[slots])

    image_message = message(product(q0, own_high[...], own_low[...]), [dots(z0_own, q0)])

    far_cut = (slots - near) // 3

    def far_mark(i):
        mark_slot(lax.rem(c + near + i, slots))

    def send_first():
        edge_peers(
            lambda index, row, col, slot: q_copy(
                index, row, col, jnp.where(row > r, c - cols + halo, halo + cols + c)
            ).start()
        )
        loop(cols, lambda i: q_copy(slots, r, col_peer(i), own, slots).start(), 1)
        loop(far_cut, far_mark)

    def first_slab(i):
        z_first[i] = first_z(halo + i)

    def take_first():
        loop(cols, first_slab)
        edge_peers(lambda index, row, col, slot: q_copy(index, row, col, slot).wait_recv())
        q_done().wait_recv()

    sums = total(
        1, image_message, send_first, lambda: loop(slots - near, far_mark, far_cut), take_first
    )

    curve0 = sums[:, width : width + 1]
    alpha0 = rz0 / curve0
    u1 = u0 - alpha0 * sums[:, :width]
    w1 = product(u1, core_high[...], core_low[...])

    def next_r(slot):
        return data[slot, PTS:, :] - alpha0 * q_first[slot]

    def next_z(slot):
        return next_r(slot) - product(w1, mark_high[slot], mark_low[slot])

    image = apply_near(next_z)
    z1_own = near_z[halo]
    r1_own = next_r(own)
    q_send[1] = image
    q_next[c] = image

    def q2_copy(peer, slot):
        return pltpu.make_async_remote_copy(
            src_ref=q_send.at[1],
            dst_ref=q_next.at[slot],
            send_sem=q2_send_sem.at[0],
            recv_sem=q2_recv_sem.at[0],
            device_id=target(r, peer),
            device_id_type=MESH,
        )

    def next_slab(i):
        residual = next_r(halo + i)
        r_next[i] = residual
        z_next[i] = residual - product(w1, mark_high[halo + i], mark_low[halo + i])

    lane = lax.broadcasted_iota(jnp.int32, (outs, 128), 1)
    line = lax.broadcasted_iota(jnp.int32, (outs, 128), 0)

    def small_copy(peer, slot):
        return pltpu.make_async_remote_copy(
            src_ref=small_send,
            dst_ref=small_recv.at[slot],
            send_sem=part_send_sem.at[2],
            recv_sem=part_recv_sem.at[2],
            device_id=target(r, peer),
            device_id_type=MESH,
        )

    def last_copy(peer, slot):
        return pltpu.make_async_remote_copy(
            src_ref=last_send,
            dst_ref=last_recv.at[slot],
            send_sem=row_send_sem.at[2],
            recv_sem=row_recv_sem.at[2],
            device_id=target(peer, c),
            device_id_type=MESH,
        )

    packed = jnp.zeros((outs, 128), F32)
    for index, scalar in enumerate(
        [dots(r1_own, z1_own), dots(z1_own, image), dots(z1_own, q0) + dots(z0_own, image)]
    ):
        packed = jnp.where(lane == line + index * outs, scalar, packed)
    packed = jnp.sum(packed, axis=0, keepdims=True)
    small_send[...] = packed
    small_recv[c] = packed
    loop(cols, lambda i: small_copy(col_peer(i), c).start(), 1)
    loop(cols, lambda i: q2_copy(col_peer(i), c).start(), 1)
    loop(cols // 2, next_slab)
    small_done = bulk(
        small_recv.at[pl.ds(0, cols - 1)], part_send_sem.at[2], part_recv_sem.at[2]
    )
    small_done.wait_recv()
    packed = jnp.sum(small_recv[...], axis=0)
    last_send[...] = packed
    last_recv[r] = packed
    loop(rows, lambda i: last_copy(row_peer(i), r).start(), 1)
    loop(cols, next_slab, cols // 2)
    q2_done = bulk(q_next.at[pl.ds(0, cols - 1)], q2_send_sem.at[0], q2_recv_sem.at[0])
    q2_done.wait_recv()
    last_done = bulk(last_recv.at[pl.ds(0, rows - 1)], row_send_sem.at[2], row_recv_sem.at[2])
    last_done.wait_recv()
    whole = jnp.sum(last_recv[...], axis=0)

    def taken(index):
        picked_lane = jnp.where(lane == line + index * outs, whole, 0.0)
        return jnp.sum(picked_lane, axis=1, keepdims=True)

    rz1 = taken(0)
    beta = rz1 / rz0
    curve1 = taken(1) + beta * (taken(2) + beta * curve0)
    alpha1 = rz1 / curve1

    def finish(i):
        at = pl.ds(pl.multiple_of(i * width, width), width)
        first = z_first[i]
        sol_out[:, at] = alpha0 * first + alpha1 * (z_next[i] + beta * first)
        res_out[:, at] = r_next[i] - alpha1 * (q_next[i] + beta * q_first[halo + i])

    loop(cols, finish)

    for k in range(2):
        part_done(k).wait_send()
        row_done(k).wait_send()
        all_done(k).wait_send()
    small_done.wait_send()
    last_done.wait_send()
    edge_peers(lambda index, row, col, slot: q_copy(index, row, col, slot).wait_send())
    q_done().wait_send()
    q2_done.wait_send()
    mark_copy(row_peer(1), r, 0).wait_send()
    mark_copy(row_peer(rows - 1), r, 1).wait_send()
    marks_done().wait_send()

    @pl.when(r < rows - 1)
    def _():
        halo_right().wait_send()

    @pl.when(r > 0)
    def _():
        halo_left().wait_send()


def body(points, targets, landmarks, neighbours, counts, core_inverse):
    cols = lax.axis_size("cols")
    rows = lax.axis_size("rows")
    row_index = lax.axis_index("rows")
    slab = points.shape[1]
    block = slab // neighbours.shape[0]
    width = slab // cols
    outs = targets.shape[0]
    land = landmarks.shape[0]
    halo = -(-REACH * block // width)
    near = 2 * halo + 1
    slots = cols + 2 * halo

    local_ids = landmarks - row_index * slab
    present = (local_ids >= 0) & (local_ids < slab)
    picked = jnp.take(points, jnp.clip(local_ids, 0, slab - 1), axis=1)
    picked = jnp.where(present[None, :], picked, 0.0)
    picked = jnp.concatenate([picked, jnp.zeros((1, land), F32)], axis=0)
    close = (local_ids >= -slab) & (local_ids < 2 * slab)
    close = jnp.broadcast_to(close[None, :].astype(F32), (8, land))
    lines = PTS + outs
    data = jnp.concatenate([points, jnp.zeros((PTS - 3, slab), F32), targets], axis=0)
    data = data.reshape(lines, cols, width).transpose(1, 0, 2)

    vmem = pltpu.VMEM
    dma = pltpu.SemaphoreType.DMA
    group = outs // cols
    wide = land + 128
    scratch = [
        vmem((slots, lines, width), F32),
        vmem((rows, 4, land), F32),
        vmem((width, PTS), F32),
        vmem((near, width, width), BF16),
        vmem((near, width, width), BF16),
        vmem((slots, land, width), BF16),
        vmem((slots, land, width), BF16),
        vmem((width, land), BF16),
        vmem((width, land), BF16),
        vmem((land, land), BF16),
        vmem((land, land), BF16),
        vmem((near, outs, width), F32),
        vmem((cols, outs, width), F32),
        vmem((cols, outs, width), F32),
        vmem((cols, outs, width), F32),
        vmem((2, outs, width), F32),
        vmem((slots, outs, width), F32),
        vmem((cols, outs, width), F32),
        vmem((2, cols, group, wide), F32),
        vmem((2, cols, group, wide), F32),
        vmem((2, group, wide), F32),
        vmem((2, rows, group, wide), F32),
        vmem((2, group, wide), F32),
        vmem((2, cols, group, wide), F32),
        vmem((1, 128), F32),
        vmem((cols, 1, 128), F32),
        vmem((1, 128), F32),
        vmem((rows, 1, 128), F32),
        dma((2,)),
        dma((2,)),
        dma((3,)),
        dma((3,)),
        dma((slots + 1,)),
        dma((slots + 1,)),
        dma((1,)),
        dma((1,)),
        dma((3,)),
        dma((3,)),
        dma((3,)),
        dma((3,)),
        dma((2,)),
        dma((2,)),
    ]
    shape = jax.ShapeDtypeStruct((outs, slab), F32)
    return tuple(
        pl.pallas_call(
            functools.partial(solve_kernel, rows, cols, halo),
            out_shape=(shape, shape),
            in_specs=[pl.BlockSpec(memory_space=pltpu.VMEM)] * 4,
            out_specs=[pl.BlockSpec(memory_space=pltpu.VMEM)] * 2,
            scratch_shapes=scratch,
            compiler_params=pltpu.CompilerParams(
                collective_id=0,
                has_side_effects=True,
                vmem_limit_bytes=48 * 1024 * 1024,
            ),
        )(data, picked, close, core_inverse)
    )


def solution(mesh):
    placed = (P(None, "rows"), P(None, "rows"), P(), P("rows", None), P("rows"), P())
    return jax.shard_map(
        body,
        mesh=mesh,
        in_specs=placed,
        out_specs=(P(None, "rows"), P(None, "rows")),
        check_vma=False,
    )
```
